128 devices in a mesh: wide: 32 (over z, y_hi, x), narrow: 4 (over y_lo, core).
Axes of the slice: x: 4, y: 4 (y_hi: 2, y_lo: 2; y = y_hi * 2 + y_lo), z: 4, core: 2. Of those that a mesh axis runs over, the one named last changes fastest.
Arguments:
- spectra: bfloat16 [2, 128, 64, 32, 256], P(None, ('wide', 'narrow')), may hold values from -6 to 6
- out_grads: bfloat16 [2, 128, 64, 32, 256], P(None, ('wide', 'narrow')), may hold values from -0.375 to 0.375
- weights: float32 [2, 64, 32, 256, 256], P(None, 'wide', 'narrow'), may hold values from -6 to 6
- mode_factor: float32 [64, 8], replicated, may hold values from -2 to 2
- in_factor: float32 [256, 64], replicated, may hold values from -0.75 to 0.75
- out_factor: float32 [256, 64], replicated, may hold values from -0.75 to 0.75
- first_moment: float32 [2, 8, 32, 4096], P(None, None, 'narrow', 'wide'), may hold values from -60 to 60
- second_moment: float32 [8, 32, 4096], P(None, 'narrow', 'wide'), may hold values from 20 to 500
Outputs:
- new_weights: float32 [2, 64, 32, 256, 256], P(None, 'wide', 'narrow')
- new_first: float32 [2, 8, 32, 4096], P(None, None, 'narrow', 'wide')
- new_second: float32 [8, 32, 4096], P(None, 'narrow', 'wide')
The draws below stay inside these ranges and needn't reach their ends.
All inputs are finite; a program needn't handle non-finite values.
Results may differ from the reference program's by a relative error of at most 0.0003.
Values may be sent and summed in bfloat16 or wider, within the bound.
No kernel may reach another device: no remote copies, remote signals or barrier semaphores. Data moves between devices by JAX's collectives and lax.ppermute only.
A program may use at most 128 MiB of HBM per device.

```python
import math
import jax
import jax.numpy as jnp
from jax import lax

KX = 64
KY = 32
C = 256
RX = 8
RI = 64
RO = 64
STEP = 1000
SAMPLES = 128


def block_scale(rng, extent, pieces, smallest, largest):
    loudness = 1.0
    for axis_at, blocks in pieces:
        heights = jax.random.uniform(jax.random.fold_in(jax.random.fold_in(rng, 6), axis_at), (blocks,), jnp.float32, smallest / len(pieces), largest / len(pieces))
        loudness = loudness * jnp.repeat(jnp.exp(heights), extent[axis_at] // blocks).reshape((-1,) + (1,) * (len(extent) - 1 - axis_at))
    return loudness


def gaussian(key, shape, deviation, reach, cuts=(), kind=jnp.bfloat16):
    entries = deviation * jax.random.normal(key, shape, jnp.float32)
    if cuts:
        entries = entries * block_scale(key, shape, cuts, -0.22, 0.18)
    return jnp.clip(entries, -reach, reach).astype(kind)


def setup_inputs(seed: int = 0) -> dict:
    arg_keys = jax.random.split(jax.random.key(seed), 9)
    return {
        "spectra": gaussian(arg_keys[0], (2, SAMPLES, KX, KY, C), 1.0, 6.0, ((1, 128),)),
        "out_grads": gaussian(arg_keys[1], (2, SAMPLES, KX, KY, C), (2 * SAMPLES) ** -0.5, 0.375, ((1, 128),)),
        "weights": gaussian(arg_keys[2], (2, KX, KY, C, C), 1.0, 6.0, ((1, 32), (2, 4)), jnp.float32),
        "mode_factor": gaussian(arg_keys[3], (KX, RX), RX ** -0.5, 2.0, (), jnp.float32),
        "in_factor": gaussian(arg_keys[4], (C, RI), RI ** -0.5, 0.75, (), jnp.float32),
        "out_factor": gaussian(arg_keys[5], (C, RO), RO ** -0.5, 0.75, (), jnp.float32),
        "first_moment": gaussian(arg_keys[6], (2, RX, KY, RI * RO), 10.0, 60.0, ((2, 4), (3, 32)), jnp.float32),
        "second_moment": jnp.clip(jnp.exp(math.log(500.0) - 3.218876 * jax.random.uniform(arg_keys[7], (RX, KY, RI * RO), jnp.float32) ** block_scale(arg_keys[7], (RX, KY, RI * RO), ((1, 4), (2, 32)), -0.2, 0.2)), 20.0, 500.0),
    }


highest = lax.Precision.HIGHEST

def reference(spectra, out_grads, weights, mode_factor, in_factor, out_factor, first_moment, second_moment):

    def project_row(operands):
        spectra_row, grads_row = operands
        products = jnp.einsum('pbmi,qbmo->pqmio', spectra_row.astype(jnp.float32), grads_row.astype(jnp.float32))
        grad = jnp.stack([products[0, 0] + products[1, 1], products[0, 1] - products[1, 0]])
        half_core = jnp.einsum('pmio,oc->pmic', grad, out_factor, precision=highest)
        return jnp.einsum('ia,pmic->pmac', in_factor, half_core, precision=highest)
    channel_core = lax.map(project_row, (jnp.moveaxis(spectra, 2, 0), jnp.moveaxis(out_grads, 2, 0)))
    core_grad = jnp.einsum('xr,xpmac->prmac', mode_factor, channel_core, precision=highest)
    core_grad = core_grad.reshape(2, RX, KY, RI * RO)
    new_first = 0.9 * first_moment + 0.1 * core_grad
    new_second = 0.999 * second_moment + 0.001 * (core_grad[0] * core_grad[0] + core_grad[1] * core_grad[1])
    first_scale = 1.0 / (1.0 - 0.9 ** STEP)
    second_scale = 1.0 / (1.0 - 0.999 ** STEP)
    core_step = new_first * first_scale / (jnp.sqrt(new_second * second_scale) + 1e-08)
    expanded = jnp.einsum('xr,prmk->xpmk', mode_factor, core_step, precision=highest)
    expanded = expanded.reshape(KX, 2, KY, RI, RO)

    def expand_row(operands):
        weight_row, expanded_row = operands
        left_part = jnp.einsum('pmac,oc->pmao', expanded_row, out_factor, precision=highest)
        change = jnp.einsum('ia,pmao->pmio', in_factor, left_part, precision=highest)
        return weight_row - 0.3 * change
    updated = lax.map(expand_row, (jnp.moveaxis(weights, 1, 0), expanded))
    new_weights = jnp.moveaxis(updated, 0, 1)
    return (new_weights, new_first, new_second)
```

```python
import jax
import jax.numpy as jnp
from jax import lax
from jax.experimental import pallas as pl
from jax.experimental.pallas import tpu as pltpu
from jax.sharding import PartitionSpec as P

STEP = 1000
F32 = jnp.float32
BF16 = jnp.bfloat16

GRAD_SCALE = 16.0
FLOOR = 2.0**-12
EDGE = 125.0
SLOPE = 250.0 / 22.2


def encode(v):
    power = jnp.exp2(SLOPE * jnp.log2(1.0 + jnp.abs(v) * (1.0 / FLOOR)) - EDGE)
    return jnp.where(v < 0, -power, power).astype(BF16)


def decode(code):
    y = code.astype(F32)
    size = jnp.exp2((jnp.log2(jnp.abs(y)) + EDGE) * (1.0 / SLOPE)) - 1.0
    return jnp.where(y < 0, -size, size)


def split(v):
    high = v.astype(BF16)
    return high, (v - high.astype(F32)).astype(BF16)


def dot(a, b, dims):
    return lax.dot_general(a, b, (dims, ((), ())), preferred_element_type=F32)


NN = ((1,), (0,))
NT = ((1,), (1,))
TN = ((0,), (0,))


def paired_rows(ref, held):
    half = ref.shape[0] // 2
    for c in range(2):
        held[c] = ref[:, c * 128 : c * 128 + 128]
    return jnp.concatenate(
        [
            jnp.concatenate([held[c, pl.ds(k, half, stride=2), :] for c in range(2)], axis=1)
            for k in range(2)
        ],
        axis=0,
    )


def project_kernel(x_ref, g_ref, in_ref, out_ref, sent_ref, factors, held):
    rows_first = x_ref.shape[1]
    narrow = x_ref.shape[2] // 8

    @pl.when(pl.program_id(0) == 0)
    def _():
        for side, factor in ((0, paired_rows(in_ref, held)), (1, GRAD_SCALE * out_ref[...])):
            high, low = split(factor)
            none = jnp.zeros_like(high)
            factors[2 * side] = jnp.concatenate([high, none, low, none], axis=0)
            factors[2 * side + 1] = jnp.concatenate([none, high, none, low], axis=0)

    for side, ref in ((0, x_ref), (1, g_ref)):
        modes = rows_first * ref.shape[2]
        real = ref[0].reshape(modes, ref.shape[3])
        imag = ref[1].reshape(modes, ref.shape[3])
        both = dot(real, factors[2 * side], NT) + dot(imag, factors[2 * side + 1], NT)
        code = encode(both[:, :128] + both[:, 128:])
        code = code.reshape(rows_first // 2, 2, narrow, 8, 128)
        for w in range(rows_first // 2):
            for n in range(narrow):
                block = jnp.concatenate([code[w, 0, n], code[w, 1, n]], axis=0)
                sent_ref[w * narrow + n, :, side * 128 : side * 128 + 128] = block


def product_kernel(got_ref, core_ref, values):
    samples, modes, lanes = got_ref.shape
    step = 16

    @pl.loop(0, samples // step)
    def _(i):
        block = got_ref[pl.ds(i * step, step)].reshape(step * modes, lanes)
        plain = decode(block)
        for c in range(2):
            values[c, pl.ds(i * step * modes, step * modes), :] = plain[:, c * 128 : c * 128 + 128]

    wide = core_ref.shape[0] // (2 * modes)
    for m in range(modes):
        s_high, s_low = split(values[0, pl.ds(m, samples, stride=modes), :])
        g_high, g_low = split(values[1, pl.ds(m, samples, stride=modes), :])
        left = jnp.concatenate([s_high, s_low], axis=1)
        right = jnp.concatenate([g_high, g_low], axis=1)
        full = dot(left, right, TN)
        core = (full[128:, 128:] + full[:128, 128:]) + full[128:, :128] + full[:128, :128]
        real = core[:64, :64] + core[64:, 64:]
        imag = core[:64, 64:] - core[64:, :64]
        for p, part in ((0, real), (1, imag)):
            tile = jnp.concatenate([part[:32], part[32:]], axis=1) * (FLOOR * FLOOR / GRAD_SCALE)
            core_ref[pl.ds(p * modes + m, wide, stride=2 * modes), :] = tile


def adam_kernel(mode_ref, core_ref, first_ref, second_ref, step_ref, new_first_ref, new_second_ref):
    ranks = mode_ref.shape[0]
    wide = core_ref.shape[0]
    zero = jnp.zeros((8, 128), F32)

    def gather(w, total):
        total = list(total)
        for k in range(2):
            for r in range(ranks):
                factor = mode_ref[r, 2 * w + k]
                for p in range(2):
                    at = p * ranks + r
                    total[at] = total[at] + factor * core_ref[w, pl.ds(16 * p + 8 * k, 8), :]
        return tuple(total)

    total = lax.fori_loop(0, wide, gather, (zero,) * (2 * ranks), unroll=4)
    first_scale = 1.0 / (1.0 - 0.9**STEP)
    second_scale = 1.0 / (1.0 - 0.999**STEP)
    steps = [None] * (2 * ranks)
    for r in range(ranks):
        real, imag = total[r], total[ranks + r]
        second = 0.999 * second_ref[r] + 0.001 * (real * real + imag * imag)
        new_second_ref[r] = second
        below = jnp.sqrt(second * second_scale) + 1e-08
        for p, grad in ((0, real), (1, imag)):
            first = 0.9 * first_ref[p, r] + 0.1 * grad
            new_first_ref[p, r] = first
            steps[p * ranks + r] = first * first_scale / below

    def expand(w, carry):
        for k in range(2):
            parts = [zero, zero]
            for r in range(ranks):
                factor = mode_ref[r, 2 * w + k]
                for p in range(2):
                    parts[p] = parts[p] + factor * steps[p * ranks + r]
            for p in range(2):
                step_ref[w, pl.ds(16 * p + 8 * k, 8), :] = parts[p]
        return carry

    lax.fori_loop(0, wide, expand, 0, unroll=4)


def change_kernel(step_ref, in_ref, out_ref, weights_ref, new_ref, right, left, held):
    count = weights_ref.shape[0]
    wide = step_ref.shape[0] // 32
    at = pl.program_id(0)

    @pl.when(at == 0)
    def _():
        high, low = split(out_ref[...])
        none = jnp.zeros_like(high)
        for half, part in ((0, high), (1, low)):
            right[half, :, :256] = jnp.concatenate([part, none], axis=0)
            right[half, :, 256:] = jnp.concatenate([none, part], axis=0)
        high, low = split(paired_rows(in_ref, held))
        left[...] = jnp.concatenate([high, high, low], axis=0)

    rows = jnp.concatenate(
        [step_ref[pl.ds(at * count + j, wide, stride=32), :] for j in range(count)], axis=0
    )
    high, low = split(rows)
    half = dot(high, right[1], NN) + dot(low, right[0], NN) + dot(high, right[0], NN)
    for j in range(count):
        one = half[j * wide : (j + 1) * wide]
        high, low = split(jnp.concatenate([one[:, :256], one[:, 256:]], axis=0))
        stacked = jnp.concatenate([high, low, high], axis=0)
        new_ref[j] = weights_ref[j] - 0.3 * dot(left[...], stacked, TN)


def whole(*shape):
    return pl.BlockSpec(shape, lambda *_: (0,) * len(shape))


def local(
    spectra, out_grads, weights, mode_factor, in_factor, out_factor, first_moment, second_moment
):
    wide = lax.axis_size("wide")
    narrow = lax.axis_size("narrow")
    _, _, modes_first, modes_second, channels = spectra.shape
    ranks = mode_factor.shape[1]
    modes = (modes_first // wide) * (modes_second // narrow)
    in_rows = in_factor.T
    out_rows = out_factor.T
    mode_rows = mode_factor.T
    parts = 8
    rows_first = modes_first // parts

    source = pl.BlockSpec(
        (2, None, rows_first, modes_second, channels), lambda i: (0, 0, i, 0, 0)
    )
    sent = pl.pallas_call(
        project_kernel,
        grid=(parts,),
        in_specs=[source, source, whole(64, channels), whole(64, channels)],
        out_specs=pl.BlockSpec((wide * narrow // parts, modes, 256), lambda i: (i, 0, 0)),
        out_shape=jax.ShapeDtypeStruct((wide * narrow, modes, 256), BF16),
        scratch_shapes=[pltpu.VMEM((4, 256, channels), BF16), pltpu.VMEM((2, 64, 128), F32)],
        name="project",
    )(spectra, out_grads, in_rows, out_rows)
    got = lax.all_to_all(sent, ("wide", "narrow"), split_axis=0, concat_axis=0, tiled=True)
    samples = got.shape[0]
    core = pl.pallas_call(
        product_kernel,
        out_shape=jax.ShapeDtypeStruct((wide * 2 * modes, 128), F32),
        scratch_shapes=[pltpu.VMEM((2, samples * modes, 128), F32)],
        name="product",
    )(got)
    core = core.reshape(wide, 2 * modes, 128)
    core = lax.all_to_all(core, "wide", split_axis=0, concat_axis=0, tiled=True)
    vmem = pl.BlockSpec(memory_space=pltpu.VMEM)
    step, new_first, new_second = pl.pallas_call(
        adam_kernel,
        in_specs=[pl.BlockSpec(memory_space=pltpu.SMEM), vmem, vmem, vmem],
        out_specs=[vmem, vmem, vmem],
        out_shape=[
            jax.ShapeDtypeStruct(core.shape, F32),
            jax.ShapeDtypeStruct(first_moment.shape, F32),
            jax.ShapeDtypeStruct(second_moment.shape, F32),
        ],
        name="adam",
    )(mode_rows, core, first_moment, second_moment)
    step = lax.all_to_all(step, "wide", split_axis=0, concat_axis=0, tiled=True)
    flat = weights.reshape(2 * modes, channels, channels)
    count = 4
    block = pl.BlockSpec((count, channels, channels), lambda i: (i, 0, 0))
    new_weights = pl.pallas_call(
        change_kernel,
        grid=(2 * modes // count,),
        in_specs=[whole(wide * 2 * modes, 128), whole(64, channels), whole(64, channels), block],
        out_specs=block,
        out_shape=jax.ShapeDtypeStruct(flat.shape, F32),
        scratch_shapes=[
            pltpu.VMEM((2, 128, 512), BF16),
            pltpu.VMEM((192, channels), BF16),
            pltpu.VMEM((2, 64, 128), F32),
        ],
        name="change",
    )(step.reshape(wide * 2 * modes, 128), in_rows, out_rows, flat)
    return (new_weights.reshape(weights.shape), new_first, new_second)


def solution(mesh):
    placed = (
        P(None, ("wide", "narrow"), None, None, None),
        P(None, ("wide", "narrow"), None, None, None),
        P(None, "wide", "narrow", None, None),
        P(),
        P(),
        P(),
        P(None, None, "narrow", "wide"),
        P(None, "narrow", "wide"),
    )
    return jax.shard_map(
        local,
        mesh=mesh,
        in_specs=placed,
        out_specs=(
            P(None, "wide", "narrow", None, None),
            P(None, None, "narrow", "wide"),
            P(None, "narrow", "wide"),
        ),
        check_vma=False,
    )
```

```python
import jax
import jax.numpy as jnp
from jax import lax
from jax.experimental import pallas as pl
from jax.experimental.pallas import tpu as pltpu
from jax.sharding import PartitionSpec as P

STEP = 1000
F32 = jnp.float32
BF16 = jnp.bfloat16

GRAD_SCALE = 16.0
FLOOR = 2.0**-12
EDGE = 125.0
SLOPE = 250.0 / 22.2


def encode(v):
    power = jnp.exp2(SLOPE * jnp.log2(1.0 + jnp.abs(v) * (1.0 / FLOOR)) - EDGE)
    return jnp.where(v < 0, -power, power).astype(BF16)


def decode(code):
    y = code.astype(F32)
    size = jnp.exp2((jnp.log2(jnp.abs(y)) + EDGE) * (1.0 / SLOPE)) - 1.0
    return jnp.where(y < 0, -size, size)


def split(v):
    high = v.astype(BF16)
    return high, (v - high.astype(F32)).astype(BF16)


def dot(a, b, dims):
    return lax.dot_general(a, b, (dims, ((), ())), preferred_element_type=F32)


NN = ((1,), (0,))
TN = ((0,), (0,))


def paired_rows(ref, held):
    half = ref.shape[0] // 2
    for c in range(2):
        held[c] = ref[:, c * 128 : c * 128 + 128]
    return jnp.concatenate(
        [
            jnp.concatenate([held[c, pl.ds(k, half, stride=2), :] for c in range(2)], axis=1)
            for k in range(2)
        ],
        axis=0,
    )


def project_kernel(
    x_hbm, g_hbm, in_hbm_ref, out_hbm_ref, sent_ref, sources, rows, factors, held, sems, row_sems
):
    parts = sems.shape[1]
    rows_first = sources.shape[2] // parts
    modes_second, channels = sources.shape[3:]
    narrow = modes_second // 8
    modes = rows_first * modes_second

    def fetch(side, i):
        at = pl.ds(i * rows_first, rows_first)
        hbm = (x_hbm, g_hbm)[side]
        return pltpu.make_async_copy(hbm.at[:, 0, at], sources.at[side, :, at], sems.at[side, i])

    def fetch_rows(side):
        hbm = (in_hbm_ref, out_hbm_ref)[side]
        return pltpu.make_async_copy(hbm, rows.at[side], row_sems.at[side])

    for side in range(2):
        fetch_rows(side).start()
    ahead = 1
    for i in range(ahead):
        for side in range(2):
            fetch(side, i).start()
    for side in range(2):
        fetch_rows(side).wait()
        factor = GRAD_SCALE * rows[1] if side else paired_rows(rows.at[0], held)
        high, low = split(factor)
        none = jnp.zeros_like(high)
        factors[2 * side] = jnp.concatenate([high, none, low, none], axis=0).T
        factors[2 * side + 1] = jnp.concatenate([none, high, none, low], axis=0).T

    @pl.loop(0, parts)
    def _(i):
        for side in range(2):
            fetch(side, i).wait()

            @pl.when(i + ahead < parts)
            def _():
                fetch(side, i + ahead).start()

            at = pl.ds(i * rows_first, rows_first)
            real = sources[side, 0, at].reshape(modes, channels)
            imag = sources[side, 1, at].reshape(modes, channels)
            both = dot(real, factors[2 * side], NN) + dot(imag, factors[2 * side + 1], NN)
            code = encode(both[:, :128] + both[:, 128:])
            code = code.reshape(rows_first // 2, 2, narrow, 8, 128)
            for w in range(rows_first // 2):
                for n in range(narrow):
                    block = jnp.concatenate([code[w, 0, n], code[w, 1, n]], axis=0)
                    dest = i * (rows_first // 2 * narrow) + w * narrow + n
                    sent_ref[dest, :, side * 128 : side * 128 + 128] = block


def product_kernel(got_ref, core_ref, values):
    samples, modes, lanes = got_ref.shape
    step = 16

    @pl.loop(0, samples // step)
    def _(i):
        block = got_ref[pl.ds(i * step, step)].reshape(step * modes, lanes)
        plain = decode(block)
        for c in range(2):
            values[c, pl.ds(i * step * modes, step * modes), :] = plain[:, c * 128 : c * 128 + 128]

    wide = core_ref.shape[0] // (2 * modes)
    for m in range(modes):
        s_high, s_low = split(values[0, pl.ds(m, samples, stride=modes), :])
        g_high, g_low = split(values[1, pl.ds(m, samples, stride=modes), :])
        left = jnp.concatenate([s_high, s_low], axis=1)
        right = jnp.concatenate([g_high, g_low], axis=1)
        full = dot(left, right, TN)
        core = (full[128:, 128:] + full[:128, 128:]) + full[128:, :128] + full[:128, :128]
        real = core[:64, :64] + core[64:, 64:]
        imag = core[:64, 64:] - core[64:, :64]
        for p, part in ((0, real), (1, imag)):
            tile = jnp.concatenate([part[:32], part[32:]], axis=1) * (FLOOR * FLOOR / GRAD_SCALE)
            core_ref[pl.ds(p * modes + m, wide, stride=2 * modes), :] = tile


def adam_kernel(
    mode_ref,
    core_ref,
    first_ref,
    second_ref,
    step_ref,
    first_hbm,
    second_hbm,
    new_first_ref,
    new_second_ref,
    sems,
):
    ranks = mode_ref.shape[0]
    wide = core_ref.shape[0]
    zero = jnp.zeros((8, 128), F32)

    def gather(w, total):
        total = list(total)
        for k in range(2):
            for r in range(ranks):
                factor = mode_ref[r, 2 * w + k]
                for p in range(2):
                    at = p * ranks + r
                    total[at] = total[at] + factor * core_ref[w, pl.ds(16 * p + 8 * k, 8), :]
        return tuple(total)

    total = lax.fori_loop(0, wide, gather, (zero,) * (2 * ranks), unroll=4)
    first_scale = 1.0 / (1.0 - 0.9**STEP)
    second_scale = 1.0 / (1.0 - 0.999**STEP)
    steps = [None] * (2 * ranks)
    for r in range(ranks):
        real, imag = total[r], total[ranks + r]
        second = 0.999 * second_ref[r] + 0.001 * (real * real + imag * imag)
        new_second_ref[r] = second
        below = jnp.sqrt(second * second_scale) + 1e-08
        for p, grad in ((0, real), (1, imag)):
            first = 0.9 * first_ref[p, r] + 0.1 * grad
            new_first_ref[p, r] = first
            steps[p * ranks + r] = first * first_scale / below

    copies = [
        pltpu.make_async_copy(new_first_ref, first_hbm, sems.at[0]),
        pltpu.make_async_copy(new_second_ref, second_hbm, sems.at[1]),
    ]
    for copy in copies:
        copy.start()

    def expand(w, carry):
        for k in range(2):
            parts = [zero, zero]
            for r in range(ranks):
                factor = mode_ref[r, 2 * w + k]
                for p in range(2):
                    parts[p] = parts[p] + factor * steps[p * ranks + r]
            for p in range(2):
                step_ref[w, pl.ds(16 * p + 8 * k, 8), :] = parts[p]
        return carry

    lax.fori_loop(0, wide, expand, 0, unroll=4)
    for copy in copies:
        copy.wait()


def change_kernel(
    step_ref, in_ref, out_ref, weights_ref, new_hbm, right, left, held, changed, sems
):
    modes = weights_ref.shape[0]
    wide = step_ref.shape[0] // modes
    count = 8
    high, low = split(out_ref[...])
    none = jnp.zeros_like(high)
    for half, part in ((0, high), (1, low)):
        right[half, :, :256] = jnp.concatenate([part, none], axis=0)
        right[half, :, 256:] = jnp.concatenate([none, part], axis=0)
    high, low = split(0.3 * paired_rows(in_ref, held))
    left[...] = jnp.concatenate([high, high, low], axis=0).T

    def give(m):
        return pltpu.make_async_copy(changed.at[m], new_hbm.at[m], sems.at[m])

    @pl.loop(0, modes // count)
    def _(i):
        rows = jnp.concatenate(
            [step_ref[pl.ds(i * count + j, wide, stride=modes), :] for j in range(count)], axis=0
        )
        high, low = split(rows)
        half = dot(high, right[1], NN) + dot(low, right[0], NN) + dot(high, right[0], NN)
        for j in range(count):
            m = i * count + j
            one = half[j * wide : (j + 1) * wide]
            high, low = split(jnp.concatenate([one[:, :256], one[:, 256:]], axis=0))
            stacked = jnp.concatenate([high, low, high], axis=0)
            changed[m] = weights_ref[m] - dot(left[...], stacked, NN)
            give(m).start()

    @pl.loop(0, modes)
    def _(m):
        give(m).wait()


def in_hbm(array):
    return pltpu.with_memory_space_constraint(array, pltpu.HBM)


def local(
    spectra, out_grads, weights, mode_factor, in_factor, out_factor, first_moment, second_moment
):
    wide = lax.axis_size("wide")
    narrow = lax.axis_size("narrow")
    _, _, modes_first, modes_second, channels = spectra.shape
    ranks = mode_factor.shape[1]
    modes = (modes_first // wide) * (modes_second // narrow)
    in_rows = in_factor.T
    out_rows = out_factor.T
    mode_rows = mode_factor.T
    parts = 2
    vmem = pl.BlockSpec(memory_space=pltpu.VMEM)
    hbm = pl.BlockSpec(memory_space=pl.ANY)
    sent = pl.pallas_call(
        project_kernel,
        in_specs=[hbm] * 4,
        out_specs=vmem,
        out_shape=jax.ShapeDtypeStruct((wide * narrow, modes, 256), BF16),
        scratch_shapes=[
            pltpu.VMEM((2, 2, modes_first, modes_second, channels), BF16),
            pltpu.VMEM((2, 64, channels), F32),
            pltpu.VMEM((4, channels, 256), BF16),
            pltpu.VMEM((2, 64, 128), F32),
            pltpu.SemaphoreType.DMA((2, parts)),
            pltpu.SemaphoreType.DMA((2,)),
        ],
        name="project",
        compiler_params=pltpu.CompilerParams(vmem_limit_bytes=12 * 2**20),
    )(in_hbm(spectra), in_hbm(out_grads), in_hbm(in_rows), in_hbm(out_rows))
    got = lax.all_to_all(sent, ("wide", "narrow"), split_axis=0, concat_axis=0, tiled=True)
    samples = got.shape[0]
    core = pl.pallas_call(
        product_kernel,
        out_shape=jax.ShapeDtypeStruct((wide * 2 * modes, 128), F32),
        scratch_shapes=[pltpu.VMEM((2, samples * modes, 128), F32)],
        name="product",
        compiler_params=pltpu.CompilerParams(vmem_limit_bytes=8 * 2**20),
    )(got)
    core = core.reshape(wide, 2 * modes, 128)
    core = lax.all_to_all(core, "wide", split_axis=0, concat_axis=0, tiled=True)
    step, new_first, new_second = pl.pallas_call(
        adam_kernel,
        in_specs=[pl.BlockSpec(memory_space=pltpu.SMEM), vmem, vmem, vmem],
        out_specs=[vmem, hbm, hbm],
        out_shape=[
            jax.ShapeDtypeStruct(core.shape, F32),
            jax.ShapeDtypeStruct(first_moment.shape, F32),
            jax.ShapeDtypeStruct(second_moment.shape, F32),
        ],
        scratch_shapes=[
            pltpu.VMEM(first_moment.shape, F32),
            pltpu.VMEM(second_moment.shape, F32),
            pltpu.SemaphoreType.DMA((2,)),
        ],
        name="adam",
        compiler_params=pltpu.CompilerParams(vmem_limit_bytes=4 * 2**20),
    )(mode_rows, core, first_moment, second_moment)
    step = lax.all_to_all(step, "wide", split_axis=0, concat_axis=0, tiled=True)
    flat = weights.reshape(2 * modes, channels, channels)
    new_weights = pl.pallas_call(
        change_kernel,
        in_specs=[vmem] * 4,
        out_specs=hbm,
        out_shape=jax.ShapeDtypeStruct(flat.shape, F32),
        scratch_shapes=[
            pltpu.VMEM((2, 128, 512), BF16),
            pltpu.VMEM((channels, 192), BF16),
            pltpu.VMEM((2, 64, 128), F32),
            pltpu.VMEM(flat.shape, F32),
            pltpu.SemaphoreType.DMA((2 * modes,)),
        ],
        name="change",
        compiler_params=pltpu.CompilerParams(vmem_limit_bytes=12 * 2**20),
    )(step.reshape(wide * 2 * modes, 128), in_rows, out_rows, flat)
    return (new_weights.reshape(weights.shape), new_first, new_second)


def solution(mesh):
    placed = (
        P(None, ("wide", "narrow"), None, None, None),
        P(None, ("wide", "narrow"), None, None, None),
        P(None, "wide", "narrow", None, None),
        P(),
        P(),
        P(),
        P(None, None, "narrow", "wide"),
        P(None, "narrow", "wide"),
    )
    return jax.shard_map(
        local,
        mesh=mesh,
        in_specs=placed,
        out_specs=(
            P(None, "wide", "narrow", None, None),
            P(None, None, "narrow", "wide"),
            P(None, "narrow", "wide"),
        ),
        check_vma=False,
    )
```

```python
import jax
import jax.numpy as jnp
from jax import lax
from jax.experimental import pallas as pl
from jax.experimental.pallas import tpu as pltpu
from jax.sharding import PartitionSpec as P

STEP = 1000
F32 = jnp.float32
BF16 = jnp.bfloat16

GRAD_SCALE = 16.0
FLOOR = 2.0**-12
EDGE = 125.0
SLOPE = 250.0 / 22.2


def encode(v):
    power = jnp.exp2(SLOPE * jnp.log2(1.0 + jnp.abs(v) * (1.0 / FLOOR)) - EDGE)
    return jnp.where(v < 0, -power, power).astype(BF16)


def decode(y):
    size = jnp.exp2((jnp.log2(jnp.abs(y)) + EDGE) * (1.0 / SLOPE)) - 1.0
    return jnp.where(y < 0, -size, size)


def split(v):
    high = v.astype(BF16)
    return high, (v - high.astype(F32)).astype(BF16)


def dot(a, b, dims):
    return lax.dot_general(a, b, (dims, ((), ())), preferred_element_type=F32)


NN = ((1,), (0,))
TN = ((0,), (0,))


def paired_rows(ref, held):
    half = ref.shape[0] // 2
    for c in range(2):
        held[c] = ref[:, c * 128 : c * 128 + 128]
    return jnp.concatenate(
        [
            jnp.concatenate([held[c, pl.ds(k, half, stride=2), :] for c in range(2)], axis=1)
            for k in range(2)
        ],
        axis=0,
    )


def project_kernel(
    x_hbm, g_hbm, in_hbm_ref, out_hbm_ref, sent_ref, sources, rows, factors, held, sems, row_sems
):
    parts = sems.shape[1]
    rows_first = sources.shape[2] // parts
    modes_second, channels = sources.shape[3:]
    narrow = modes_second // 8
    modes = rows_first * modes_second

    def fetch(side, i):
        at = pl.ds(i * rows_first, rows_first)
        hbm = (x_hbm, g_hbm)[side]
        return pltpu.make_async_copy(hbm.at[:, 0, at], sources.at[side, :, at], sems.at[side, i])

    def fetch_rows(side):
        hbm = (in_hbm_ref, out_hbm_ref)[side]
        return pltpu.make_async_copy(hbm, rows.at[side], row_sems.at[side])

    for side in range(2):
        fetch_rows(side).start()
    ahead = 1
    for i in range(ahead):
        for side in range(2):
            fetch(side, i).start()
    for side in range(2):
        fetch_rows(side).wait()
        factor = GRAD_SCALE * rows[1] if side else paired_rows(rows.at[0], held)
        high, low = split(factor)
        none = jnp.zeros_like(high)
        factors[2 * side] = jnp.concatenate([high, none, low, none], axis=0).T
        factors[2 * side + 1] = jnp.concatenate([none, high, none, low], axis=0).T

    @pl.loop(0, parts)
    def _(i):
        for side in range(2):
            fetch(side, i).wait()

            @pl.when(i + ahead < parts)
            def _():
                fetch(side, i + ahead).start()

            at = pl.ds(i * rows_first, rows_first)
            real = sources[side, 0, at].reshape(modes, channels)
            imag = sources[side, 1, at].reshape(modes, channels)
            both = dot(real, factors[2 * side], NN) + dot(imag, factors[2 * side + 1], NN)
            code = encode(both[:, :128] + both[:, 128:])
            code = code.reshape(rows_first // 2, 2, narrow, 8, 128)
            for w in range(rows_first // 2):
                for n in range(narrow):
                    block = jnp.concatenate([code[w, 0, n], code[w, 1, n]], axis=0)
                    dest = i * (rows_first // 2 * narrow) + w * narrow + n
                    sent_ref[dest, :, side * 128 : side * 128 + 128] = block


def product_kernel(got_ref, core_ref, values):
    samples, modes, lanes = got_ref.shape
    step = 16

    @pl.loop(0, samples // step)
    def _(i):
        block = got_ref[pl.ds(i * step, step)].reshape(step * modes, lanes)
        plain = block.astype(F32)
        for c in range(2):
            values[c, pl.ds(i * step * modes, step * modes), :] = plain[:, c * 128 : c * 128 + 128]

    wide = core_ref.shape[0] // (2 * modes)
    for m in range(modes):
        s_high, s_low = split(decode(values[0, pl.ds(m, samples, stride=modes), :]))
        g_high, g_low = split(decode(values[1, pl.ds(m, samples, stride=modes), :]))
        left = jnp.concatenate([s_high, s_low], axis=1)
        right = jnp.concatenate([g_high, g_low], axis=1)
        full = dot(left, right, TN)
        core = (full[128:, 128:] + full[:128, 128:]) + full[128:, :128] + full[:128, :128]
        real = core[:64, :64] + core[64:, 64:]
        imag = core[:64, 64:] - core[64:, :64]
        for p, part in ((0, real), (1, imag)):
            tile = jnp.concatenate([part[:32], part[32:]], axis=1) * (FLOOR * FLOOR / GRAD_SCALE)
            core_ref[pl.ds(p * modes + m, wide, stride=2 * modes), :] = tile


def adam_kernel(
    mode_ref,
    core_ref,
    first_ref,
    second_ref,
    step_ref,
    first_hbm,
    second_hbm,
    new_first_ref,
    new_second_ref,
    sems,
):
    ranks = mode_ref.shape[0]
    wide = core_ref.shape[0]
    zero = jnp.zeros((8, 128), F32)

    def gather(w, total):
        total = list(total)
        for k in range(2):
            for r in range(ranks):
                factor = mode_ref[r, 2 * w + k]
                for p in range(2):
                    at = p * ranks + r
                    total[at] = total[at] + factor * core_ref[w, pl.ds(16 * p + 8 * k, 8), :]
        return tuple(total)

    total = lax.fori_loop(0, wide, gather, (zero,) * (2 * ranks), unroll=4)
    first_scale = 1.0 / (1.0 - 0.9**STEP)
    second_scale = 1.0 / (1.0 - 0.999**STEP)
    steps = [None] * (2 * ranks)
    for r in range(ranks):
        real, imag = total[r], total[ranks + r]
        second = 0.999 * second_ref[r] + 0.001 * (real * real + imag * imag)
        new_second_ref[r] = second
        below = jnp.sqrt(second * second_scale) + 1e-08
        for p, grad in ((0, real), (1, imag)):
            first = 0.9 * first_ref[p, r] + 0.1 * grad
            new_first_ref[p, r] = first
            steps[p * ranks + r] = first * first_scale / below

    copies = [
        pltpu.make_async_copy(new_first_ref, first_hbm, sems.at[0]),
        pltpu.make_async_copy(new_second_ref, second_hbm, sems.at[1]),
    ]
    for copy in copies:
        copy.start()

    def expand(w, carry):
        for k in range(2):
            parts = [zero, zero]
            for r in range(ranks):
                factor = mode_ref[r, 2 * w + k]
                for p in range(2):
                    parts[p] = parts[p] + factor * steps[p * ranks + r]
            for p in range(2):
                step_ref[w, pl.ds(16 * p + 8 * k, 8), :] = parts[p]
        return carry

    lax.fori_loop(0, wide, expand, 0, unroll=4)
    for copy in copies:
        copy.wait()


def change_kernel(
    step_ref, in_ref, out_ref, weights_ref, new_hbm, right, left, held, changed, sems
):
    modes = weights_ref.shape[0]
    wide = step_ref.shape[0] // modes
    count = 16
    high, low = split(out_ref[...])
    none = jnp.zeros_like(high)
    for half, part in ((0, high), (1, low)):
        right[half, :, :256] = jnp.concatenate([part, none], axis=0)
        right[half, :, 256:] = jnp.concatenate([none, part], axis=0)
    high, low = split(0.3 * paired_rows(in_ref, held))
    left[...] = jnp.concatenate([high, high, low], axis=0).T

    def give(m):
        return pltpu.make_async_copy(changed.at[m], new_hbm.at[m], sems.at[m])

    @pl.loop(0, modes // count)
    def _(i):
        rows = jnp.concatenate(
            [step_ref[pl.ds(i * count + j, wide, stride=modes), :] for j in range(count)], axis=0
        )
        high, low = split(rows)
        half = dot(high, right[1], NN) + dot(low, right[0], NN) + dot(high, right[0], NN)
        for j in range(count):
            m = i * count + j
            one = half[j * wide : (j + 1) * wide]
            high, low = split(jnp.concatenate([one[:, :256], one[:, 256:]], axis=0))
            stacked = jnp.concatenate([high, low, high], axis=0)
            changed[m] = weights_ref[m] - dot(left[...], stacked, NN)
            give(m).start()

    @pl.loop(0, modes)
    def _(m):
        give(m).wait()


def in_hbm(array):
    return pltpu.with_memory_space_constraint(array, pltpu.HBM)


def local(
    spectra, out_grads, weights, mode_factor, in_factor, out_factor, first_moment, second_moment
):
    wide = lax.axis_size("wide")
    narrow = lax.axis_size("narrow")
    _, _, modes_first, modes_second, channels = spectra.shape
    ranks = mode_factor.shape[1]
    modes = (modes_first // wide) * (modes_second // narrow)
    in_rows = in_factor.T
    out_rows = out_factor.T
    mode_rows = mode_factor.T
    parts = 2
    vmem = pl.BlockSpec(memory_space=pltpu.VMEM)
    hbm = pl.BlockSpec(memory_space=pl.ANY)
    sent = pl.pallas_call(
        project_kernel,
        in_specs=[hbm] * 4,
        out_specs=vmem,
        out_shape=jax.ShapeDtypeStruct((wide * narrow, modes, 256), BF16),
        scratch_shapes=[
            pltpu.VMEM((2, 2, modes_first, modes_second, channels), BF16),
            pltpu.VMEM((2, 64, channels), F32),
            pltpu.VMEM((4, channels, 256), BF16),
            pltpu.VMEM((2, 64, 128), F32),
            pltpu.SemaphoreType.DMA((2, parts)),
            pltpu.SemaphoreType.DMA((2,)),
        ],
        name="project",
        compiler_params=pltpu.CompilerParams(vmem_limit_bytes=12 * 2**20),
    )(in_hbm(spectra), in_hbm(out_grads), in_hbm(in_rows), in_hbm(out_rows))
    got = lax.all_to_all(sent, ("wide", "narrow"), split_axis=0, concat_axis=0, tiled=True)
    samples = got.shape[0]
    core = pl.pallas_call(
        product_kernel,
        out_shape=jax.ShapeDtypeStruct((wide * 2 * modes, 128), F32),
        scratch_shapes=[pltpu.VMEM((2, samples * modes, 128), F32)],
        name="product",
        compiler_params=pltpu.CompilerParams(vmem_limit_bytes=8 * 2**20),
    )(got)
    core = core.reshape(wide, 2 * modes, 128)
    core = lax.all_to_all(core, "wide", split_axis=0, concat_axis=0, tiled=True)
    step, new_first, new_second = pl.pallas_call(
        adam_kernel,
        in_specs=[pl.BlockSpec(memory_space=pltpu.SMEM), vmem, vmem, vmem],
        out_specs=[vmem, hbm, hbm],
        out_shape=[
            jax.ShapeDtypeStruct(core.shape, F32),
            jax.ShapeDtypeStruct(first_moment.shape, F32),
            jax.ShapeDtypeStruct(second_moment.shape, F32),
        ],
        scratch_shapes=[
            pltpu.VMEM(first_moment.shape, F32),
            pltpu.VMEM(second_moment.shape, F32),
            pltpu.SemaphoreType.DMA((2,)),
        ],
        name="adam",
        compiler_params=pltpu.CompilerParams(vmem_limit_bytes=4 * 2**20),
    )(mode_rows, core, first_moment, second_moment)
    step = lax.all_to_all(step, "wide", split_axis=0, concat_axis=0, tiled=True)
    flat = weights.reshape(2 * modes, channels, channels)
    new_weights = pl.pallas_call(
        change_kernel,
        in_specs=[vmem] * 4,
        out_specs=hbm,
        out_shape=jax.ShapeDtypeStruct(flat.shape, F32),
        scratch_shapes=[
            pltpu.VMEM((2, 128, 512), BF16),
            pltpu.VMEM((channels, 192), BF16),
            pltpu.VMEM((2, 64, 128), F32),
            pltpu.VMEM(flat.shape, F32),
            pltpu.SemaphoreType.DMA((2 * modes,)),
        ],
        name="change",
        compiler_params=pltpu.CompilerParams(vmem_limit_bytes=14 * 2**20),
    )(step.reshape(wide * 2 * modes, 128), in_rows, out_rows, flat)
    return (new_weights.reshape(weights.shape), new_first, new_second)


def solution(mesh):
    placed = (
        P(None, ("wide", "narrow"), None, None, None),
        P(None, ("wide", "narrow"), None, None, None),
        P(None, "wide", "narrow", None, None),
        P(),
        P(),
        P(),
        P(None, None, "narrow", "wide"),
        P(None, "narrow", "wide"),
    )
    return jax.shard_map(
        local,
        mesh=mesh,
        in_specs=placed,
        out_specs=(
            P(None, "wide", "narrow", None, None),
            P(None, None, "narrow", "wide"),
            P(None, "narrow", "wide"),
        ),
        check_vma=False,
    )
```

```python
import jax
import jax.numpy as jnp
from jax import lax
from jax.experimental import pallas as pl
from jax.experimental.pallas import tpu as pltpu
from jax.sharding import PartitionSpec as P

STEP = 1000
F32 = jnp.float32
BF16 = jnp.bfloat16

GRAD_SCALE = 16.0
FLOOR = 2.0**-12
EDGE = 125.0
SLOPE = 250.0 / 22.2


def encode(v):
    power = jnp.exp2(SLOPE * jnp.log2(1.0 + jnp.abs(v) * (1.0 / FLOOR)) - EDGE)
    return jnp.where(v < 0, -power, power).astype(BF16)


def decode(y):
    size = jnp.exp2((jnp.log2(jnp.abs(y)) + EDGE) * (1.0 / SLOPE)) - 1.0
    return jnp.where(y < 0, -size, size)


def split(v):
    high = v.astype(BF16)
    return high, (v - high.astype(F32)).astype(BF16)


def dot(a, b, dims):
    return lax.dot_general(a, b, (dims, ((), ())), preferred_element_type=F32)


NN = ((1,), (0,))
TN = ((0,), (0,))


def paired_rows(ref, held):
    half = ref.shape[0] // 2
    for c in range(2):
        held[c] = ref[:, c * 128 : c * 128 + 128]
    return jnp.concatenate(
        [
            jnp.concatenate([held[c, pl.ds(k, half, stride=2), :] for c in range(2)], axis=1)
            for k in range(2)
        ],
        axis=0,
    )


def project_kernel(
    x_hbm, g_hbm, in_hbm_ref, out_hbm_ref, sent_ref, sources, rows, factors, held, sems, row_sems
):
    parts = sems.shape[1]
    rows_first = sources.shape[2] // parts
    modes_second, channels = sources.shape[3:]
    narrow = modes_second // 8
    modes = rows_first * modes_second

    def fetch(side, i):
        at = pl.ds(i * rows_first, rows_first)
        hbm = (x_hbm, g_hbm)[side]
        return pltpu.make_async_copy(hbm.at[:, 0, at], sources.at[side, :, at], sems.at[side, i])

    def fetch_rows(side):
        hbm = (in_hbm_ref, out_hbm_ref)[side]
        return pltpu.make_async_copy(hbm, rows.at[side], row_sems.at[side])

    for side in range(2):
        fetch_rows(side).start()
    ahead = 1
    for i in range(ahead):
        for side in range(2):
            fetch(side, i).start()
    for side in range(2):
        fetch_rows(side).wait()
        factor = GRAD_SCALE * rows[1] if side else paired_rows(rows.at[0], held)
        high, low = split(factor)
        none = jnp.zeros_like(high)
        factors[2 * side] = jnp.concatenate([high, none, low, none], axis=0).T
        factors[2 * side + 1] = jnp.concatenate([none, high, none, low], axis=0).T

    @pl.loop(0, parts)
    def _(i):
        for side in range(2):
            fetch(side, i).wait()

            @pl.when(i + ahead < parts)
            def _():
                fetch(side, i + ahead).start()

            at = pl.ds(i * rows_first, rows_first)
            real = sources[side, 0, at].reshape(modes, channels)
            imag = sources[side, 1, at].reshape(modes, channels)
            both = dot(real, factors[2 * side], NN) + dot(imag, factors[2 * side + 1], NN)
            code = encode(both[:, :128] + both[:, 128:])
            code = code.reshape(rows_first // 2, 2, narrow, 8, 128)
            for w in range(rows_first // 2):
                for n in range(narrow):
                    block = jnp.concatenate([code[w, 0, n], code[w, 1, n]], axis=0)
                    dest = i * (rows_first // 2 * narrow) + w * narrow + n
                    sent_ref[dest, :, side * 128 : side * 128 + 128] = block


def product_kernel(got_ref, core_ref, values):
    samples, modes, lanes = got_ref.shape
    step = 16

    @pl.loop(0, samples // step)
    def _(i):
        block = got_ref[pl.ds(i * step, step)].reshape(step * modes, lanes)
        plain = block.astype(F32)
        for c in range(2):
            values[c, pl.ds(i * step * modes, step * modes), :] = plain[:, c * 128 : c * 128 + 128]

    wide = core_ref.shape[0] // (2 * modes)
    for m in range(modes):
        s_high, s_low = split(decode(values[0, pl.ds(m, samples, stride=modes), :]))
        g_high, g_low = split(decode(values[1, pl.ds(m, samples, stride=modes), :]))
        left = jnp.concatenate([s_high, s_low], axis=1)
        right = jnp.concatenate([g_high, g_low], axis=1)
        full = dot(left, right, TN)
        core = (full[128:, 128:] + full[:128, 128:]) + full[128:, :128] + full[:128, :128]
        real = core[:64, :64] + core[64:, 64:]
        imag = core[:64, 64:] - core[64:, :64]
        for p, part in ((0, real), (1, imag)):
            tile = jnp.concatenate([part[:32], part[32:]], axis=1) * (FLOOR * FLOOR / GRAD_SCALE)
            core_ref[pl.ds(p * modes + m, wide, stride=2 * modes), :] = tile


def adam_kernel(
    mode_ref,
    core_ref,
    first_ref,
    second_ref,
    step_ref,
    first_hbm,
    second_hbm,
    new_first_ref,
    new_second_ref,
    sems,
):
    ranks = mode_ref.shape[0]
    wide = core_ref.shape[0]
    zero = jnp.zeros((8, 128), F32)

    def gather(w, total):
        total = list(total)
        for k in range(2):
            for r in range(ranks):
                factor = mode_ref[r, 2 * w + k]
                for p in range(2):
                    at = p * ranks + r
                    total[at] = total[at] + factor * core_ref[w, pl.ds(16 * p + 8 * k, 8), :]
        return tuple(total)

    total = lax.fori_loop(0, wide, gather, (zero,) * (2 * ranks), unroll=4)
    first_scale = 1.0 / (1.0 - 0.9**STEP)
    second_scale = 1.0 / (1.0 - 0.999**STEP)
    steps = [None] * (2 * ranks)
    for r in range(ranks):
        real, imag = total[r], total[ranks + r]
        second = 0.999 * second_ref[r] + 0.001 * (real * real + imag * imag)
        new_second_ref[r] = second
        below = jnp.sqrt(second * second_scale) + 1e-08
        for p, grad in ((0, real), (1, imag)):
            first = 0.9 * first_ref[p, r] + 0.1 * grad
            new_first_ref[p, r] = first
            steps[p * ranks + r] = first * first_scale / below

    copies = [
        pltpu.make_async_copy(new_first_ref, first_hbm, sems.at[0]),
        pltpu.make_async_copy(new_second_ref, second_hbm, sems.at[1]),
    ]
    for copy in copies:
        copy.start()

    def expand(w, carry):
        for k in range(2):
            parts = [zero, zero]
            for r in range(ranks):
                factor = mode_ref[r, 2 * w + k]
                for p in range(2):
                    parts[p] = parts[p] + factor * steps[p * ranks + r]
            for p in range(2):
                step_ref[w, pl.ds(16 * p + 8 * k, 8), :] = parts[p]
        return carry

    lax.fori_loop(0, wide, expand, 0, unroll=4)
    for copy in copies:
        copy.wait()


def change_kernel(
    step_ref, in_ref, out_ref, weights_ref, new_hbm, right, left, held, changed, sems
):
    modes = weights_ref.shape[0]
    wide = step_ref.shape[0] // modes
    count = 16
    high, low = split(out_ref[...])
    none = jnp.zeros_like(high)
    right[0] = jnp.concatenate([high, high, low, none], axis=0)
    right[1] = jnp.concatenate([high, high, none, low], axis=0)
    high, low = split(0.3 * paired_rows(in_ref, held))
    left[...] = jnp.concatenate([high, high, low], axis=0).T

    def give(m):
        return pltpu.make_async_copy(changed.at[m], new_hbm.at[m], sems.at[m])

    @pl.loop(0, modes // count)
    def _(i):
        rows = jnp.concatenate(
            [step_ref[pl.ds(i * count + j, wide, stride=modes), :] for j in range(count)], axis=0
        )
        high, _ = split(rows)
        coarse = high.astype(F32)
        turned = pltpu.roll(rows - coarse, 64, 1)
        first_half = lax.broadcasted_iota(jnp.int32, rows.shape, 1) < 64
        even, odd = (
            dot(jnp.concatenate([mixed.astype(BF16), high], axis=1), right[k], NN)
            for k, mixed in (
                (0, jnp.where(first_half, coarse, turned)),
                (1, jnp.where(first_half, turned, coarse)),
            )
        )
        for j in range(count):
            m = i * count + j
            mine = slice(j * wide, (j + 1) * wide)
            high, low = split(jnp.concatenate([even[mine], odd[mine]], axis=0))
            stacked = jnp.concatenate([high, low, high], axis=0)
            changed[m] = weights_ref[m] - dot(left[...], stacked, NN)
            give(m).start()

    @pl.loop(0, modes)
    def _(m):
        give(m).wait()


def in_hbm(array):
    return pltpu.with_memory_space_constraint(array, pltpu.HBM)


def local(
    spectra, out_grads, weights, mode_factor, in_factor, out_factor, first_moment, second_moment
):
    wide = lax.axis_size("wide")
    narrow = lax.axis_size("narrow")
    _, _, modes_first, modes_second, channels = spectra.shape
    ranks = mode_factor.shape[1]
    modes = (modes_first // wide) * (modes_second // narrow)
    in_rows = in_factor.T
    out_rows = out_factor.T
    mode_rows = mode_factor.T
    parts = 2
    vmem = pl.BlockSpec(memory_space=pltpu.VMEM)
    hbm = pl.BlockSpec(memory_space=pl.ANY)
    sent = pl.pallas_call(
        project_kernel,
        in_specs=[hbm] * 4,
        out_specs=vmem,
        out_shape=jax.ShapeDtypeStruct((wide * narrow, modes, 256), BF16),
        scratch_shapes=[
            pltpu.VMEM((2, 2, modes_first, modes_second, channels), BF16),
            pltpu.VMEM((2, 64, channels), F32),
            pltpu.VMEM((4, channels, 256), BF16),
            pltpu.VMEM((2, 64, 128), F32),
            pltpu.SemaphoreType.DMA((2, parts)),
            pltpu.SemaphoreType.DMA((2,)),
        ],
        name="project",
        compiler_params=pltpu.CompilerParams(vmem_limit_bytes=12 * 2**20),
    )(in_hbm(spectra), in_hbm(out_grads), in_hbm(in_rows), in_hbm(out_rows))
    got = lax.all_to_all(sent, ("wide", "narrow"), split_axis=0, concat_axis=0, tiled=True)
    samples = got.shape[0]
    core = pl.pallas_call(
        product_kernel,
        out_shape=jax.ShapeDtypeStruct((wide * 2 * modes, 128), F32),
        scratch_shapes=[pltpu.VMEM((2, samples * modes, 128), F32)],
        name="product",
        compiler_params=pltpu.CompilerParams(vmem_limit_bytes=8 * 2**20),
    )(got)
    core = core.reshape(wide, 2 * modes, 128)
    core = lax.all_to_all(core, "wide", split_axis=0, concat_axis=0, tiled=True)
    step, new_first, new_second = pl.pallas_call(
        adam_kernel,
        in_specs=[pl.BlockSpec(memory_space=pltpu.SMEM), vmem, vmem, vmem],
        out_specs=[vmem, hbm, hbm],
        out_shape=[
            jax.ShapeDtypeStruct(core.shape, F32),
            jax.ShapeDtypeStruct(first_moment.shape, F32),
            jax.ShapeDtypeStruct(second_moment.shape, F32),
        ],
        scratch_shapes=[
            pltpu.VMEM(first_moment.shape, F32),
            pltpu.VMEM(second_moment.shape, F32),
            pltpu.SemaphoreType.DMA((2,)),
        ],
        name="adam",
        compiler_params=pltpu.CompilerParams(vmem_limit_bytes=4 * 2**20),
    )(mode_rows, core, first_moment, second_moment)
    step = lax.all_to_all(step, "wide", split_axis=0, concat_axis=0, tiled=True)
    flat = weights.reshape(2 * modes, channels, channels)
    new_weights = pl.pallas_call(
        change_kernel,
        in_specs=[vmem] * 4,
        out_specs=hbm,
        out_shape=jax.ShapeDtypeStruct(flat.shape, F32),
        scratch_shapes=[
            pltpu.VMEM((2, 256, channels), BF16),
            pltpu.VMEM((channels, 192), BF16),
            pltpu.VMEM((2, 64, 128), F32),
            pltpu.VMEM(flat.shape, F32),
            pltpu.SemaphoreType.DMA((2 * modes,)),
        ],
        name="change",
        compiler_params=pltpu.CompilerParams(vmem_limit_bytes=14 * 2**20),
    )(step.reshape(wide * 2 * modes, 128), in_rows, out_rows, flat)
    return (new_weights.reshape(weights.shape), new_first, new_second)


def solution(mesh):
    placed = (
        P(None, ("wide", "narrow"), None, None, None),
        P(None, ("wide", "narrow"), None, None, None),
        P(None, "wide", "narrow", None, None),
        P(),
        P(),
        P(),
        P(None, None, "narrow", "wide"),
        P(None, "narrow", "wide"),
    )
    return jax.shard_map(
        local,
        mesh=mesh,
        in_specs=placed,
        out_specs=(
            P(None, "wide", "narrow", None, None),
            P(None, None, "narrow", "wide"),
            P(None, "narrow", "wide"),
        ),
        check_vma=False,
    )
```

```python
import jax
import jax.numpy as jnp
from jax import lax
from jax.experimental import pallas as pl
from jax.experimental.pallas import tpu as pltpu
from jax.sharding import PartitionSpec as P

STEP = 1000
F32 = jnp.float32
BF16 = jnp.bfloat16

GRAD_SCALE = 16.0
FLOOR = 2.0**-12
EDGE = 125.0
SLOPE = 250.0 / 22.2


def encode(v):
    power = jnp.exp2(SLOPE * jnp.log2(1.0 + jnp.abs(v) * (1.0 / FLOOR)) - EDGE)
    return jnp.where(v < 0, -power, power).astype(BF16)


def decode(y):
    size = jnp.exp2((jnp.log2(jnp.abs(y)) + EDGE) * (1.0 / SLOPE)) - 1.0
    return jnp.where(y < 0, -size, size)


def split(v):
    high = v.astype(BF16)
    return high, (v - high.astype(F32)).astype(BF16)


def dot(a, b, dims):
    return lax.dot_general(a, b, (dims, ((), ())), preferred_element_type=F32)


NN = ((1,), (0,))
TN = ((0,), (0,))


def paired_rows(ref, held):
    half = ref.shape[0] // 2
    for c in range(2):
        held[c] = ref[:, c * 128 : c * 128 + 128]
    return jnp.concatenate(
        [
            jnp.concatenate([held[c, pl.ds(k, half, stride=2), :] for c in range(2)], axis=1)
            for k in range(2)
        ],
        axis=0,
    )


def project_kernel(
    x_hbm, g_hbm, in_hbm_ref, out_hbm_ref, sent_ref, sources, rows, factors, held, sems, row_sems
):
    parts = sems.shape[1]
    rows_first = sources.shape[2] // parts
    modes_second, channels = sources.shape[3:]
    narrow = modes_second // 8

    def fetch(side, i):
        at = pl.ds(i * rows_first, rows_first)
        hbm = (x_hbm, g_hbm)[side]
        return pltpu.make_async_copy(hbm.at[:, 0, at], sources.at[side, :, at], sems.at[side, i])

    def fetch_rows(side):
        hbm = (in_hbm_ref, out_hbm_ref)[side]
        return pltpu.make_async_copy(hbm, rows.at[side], row_sems.at[side])

    for side in range(2):
        fetch_rows(side).start()
    for i in range(parts):
        fetch(0, i).start()
    for side in range(2):
        fetch_rows(side).wait()
        factor = GRAD_SCALE * rows[1] if side else paired_rows(rows.at[0], held)
        high, low = split(factor)
        none = jnp.zeros_like(high)
        factors[2 * side] = jnp.concatenate([high, none, low, none], axis=0).T
        factors[2 * side + 1] = jnp.concatenate([none, high, none, low], axis=0).T

    def emit(side, at, count, base):
        modes = count * modes_second
        real = sources[side, 0, at].reshape(modes, channels)
        imag = sources[side, 1, at].reshape(modes, channels)
        both = dot(real, factors[2 * side], NN) + dot(imag, factors[2 * side + 1], NN)
        code = encode(both[:, :128] + both[:, 128:])
        code = code.reshape(count // 2, 2, narrow, 8, 128)
        for w in range(count // 2):
            for n in range(narrow):
                block = jnp.concatenate([code[w, 0, n], code[w, 1, n]], axis=0)
                sent_ref[base + w * narrow + n, :, side * 128 : side * 128 + 128] = block

    @pl.loop(0, parts)
    def _(i):
        fetch(0, i).wait()

        @pl.when(i == 0)
        def _():
            for k in range(parts):
                fetch(1, k).start()

        emit(0, pl.ds(i * rows_first, rows_first), rows_first, i * (rows_first // 2 * narrow))

    for k in range(parts):
        fetch(1, k).wait()
    emit(1, slice(None), parts * rows_first, 0)


def product_kernel(got_ref, core_ref, values):
    samples, modes, lanes = got_ref.shape
    step = 16

    @pl.loop(0, samples // step)
    def _(i):
        block = got_ref[pl.ds(i * step, step)].reshape(step * modes, lanes)
        plain = block.astype(F32)
        for c in range(2):
            values[c, pl.ds(i * step * modes, step * modes), :] = plain[:, c * 128 : c * 128 + 128]

    wide = core_ref.shape[0] // (2 * modes)
    for m in range(modes):
        s_high, s_low = split(decode(values[0, pl.ds(m, samples, stride=modes), :]))
        g_high, g_low = split(decode(values[1, pl.ds(m, samples, stride=modes), :]))
        left = jnp.concatenate([s_high, s_low], axis=1)
        right = jnp.concatenate([g_high, g_low], axis=1)
        full = dot(left, right, TN)
        core = (full[128:, 128:] + full[:128, 128:]) + full[128:, :128] + full[:128, :128]
        real = core[:64, :64] + core[64:, 64:]
        imag = core[:64, 64:] - core[64:, :64]
        for p, part in ((0, real), (1, imag)):
            tile = jnp.concatenate([part[:32], part[32:]], axis=1) * (FLOOR * FLOOR / GRAD_SCALE)
            core_ref[pl.ds(p * modes + m, wide, stride=2 * modes), :] = tile


def adam_kernel(
    mode_ref,
    core_ref,
    first_ref,
    second_ref,
    step_ref,
    first_hbm,
    second_hbm,
    new_first_ref,
    new_second_ref,
    sems,
):
    ranks = mode_ref.shape[0]
    wide = core_ref.shape[0]
    zero = jnp.zeros((8, 128), F32)

    def gather(w, total):
        total = list(total)
        for k in range(2):
            for r in range(ranks):
                factor = mode_ref[r, 2 * w + k]
                for p in range(2):
                    at = p * ranks + r
                    total[at] = total[at] + factor * core_ref[w, pl.ds(16 * p + 8 * k, 8), :]
        return tuple(total)

    total = lax.fori_loop(0, wide, gather, (zero,) * (2 * ranks), unroll=4)
    first_scale = 1.0 / (1.0 - 0.9**STEP)
    second_scale = 1.0 / (1.0 - 0.999**STEP)
    steps = [None] * (2 * ranks)
    for r in range(ranks):
        real, imag = total[r], total[ranks + r]
        second = 0.999 * second_ref[r] + 0.001 * (real * real + imag * imag)
        new_second_ref[r] = second
        below = jnp.sqrt(second * second_scale) + 1e-08
        for p, grad in ((0, real), (1, imag)):
            first = 0.9 * first_ref[p, r] + 0.1 * grad
            new_first_ref[p, r] = first
            steps[p * ranks + r] = first * first_scale / below

    copies = [
        pltpu.make_async_copy(new_first_ref, first_hbm, sems.at[0]),
        pltpu.make_async_copy(new_second_ref, second_hbm, sems.at[1]),
    ]
    for copy in copies:
        copy.start()

    def expand(w, carry):
        for k in range(2):
            parts = [zero, zero]
            for r in range(ranks):
                factor = mode_ref[r, 2 * w + k]
                for p in range(2):
                    parts[p] = parts[p] + factor * steps[p * ranks + r]
            for p in range(2):
                step_ref[w, pl.ds(16 * p + 8 * k, 8), :] = parts[p]
        return carry

    lax.fori_loop(0, wide, expand, 0, unroll=4)
    for copy in copies:
        copy.wait()


def change_kernel(
    step_ref, in_ref, out_ref, weights_ref, new_hbm, right, left, held, changed, sems
):
    modes = weights_ref.shape[0]
    wide = step_ref.shape[0] // modes
    count = 16
    high, low = split(out_ref[...])
    none = jnp.zeros_like(high)
    right[0] = jnp.concatenate([high, high, low, none], axis=0)
    right[1] = jnp.concatenate([high, high, none, low], axis=0)
    high, low = split(0.3 * paired_rows(in_ref, held))
    left[...] = jnp.concatenate([high, high, low], axis=0).T

    def give(m):
        return pltpu.make_async_copy(changed.at[m], new_hbm.at[m], sems.at[m])

    @pl.loop(0, modes // count)
    def _(i):
        rows = jnp.concatenate(
            [step_ref[pl.ds(i * count + j, wide, stride=modes), :] for j in range(count)], axis=0
        )
        high, _ = split(rows)
        coarse = high.astype(F32)
        turned = pltpu.roll(rows - coarse, 64, 1)
        first_half = lax.broadcasted_iota(jnp.int32, rows.shape, 1) < 64
        even, odd = (
            dot(jnp.concatenate([mixed.astype(BF16), high], axis=1), right[k], NN)
            for k, mixed in (
                (0, jnp.where(first_half, coarse, turned)),
                (1, jnp.where(first_half, turned, coarse)),
            )
        )
        for j in range(count):
            m = i * count + j
            mine = slice(j * wide, (j + 1) * wide)
            high, low = split(jnp.concatenate([even[mine], odd[mine]], axis=0))
            stacked = jnp.concatenate([high, low, high], axis=0)
            changed[m] = weights_ref[m] - dot(left[...], stacked, NN)
            give(m).start()

    @pl.loop(0, modes)
    def _(m):
        give(m).wait()


def in_hbm(array):
    return pltpu.with_memory_space_constraint(array, pltpu.HBM)


def local(
    spectra, out_grads, weights, mode_factor, in_factor, out_factor, first_moment, second_moment
):
    wide = lax.axis_size("wide")
    narrow = lax.axis_size("narrow")
    _, _, modes_first, modes_second, channels = spectra.shape
    ranks = mode_factor.shape[1]
    modes = (modes_first // wide) * (modes_second // narrow)
    in_rows = in_factor.T
    out_rows = out_factor.T
    mode_rows = mode_factor.T
    parts = 2
    vmem = pl.BlockSpec(memory_space=pltpu.VMEM)
    hbm = pl.BlockSpec(memory_space=pl.ANY)
    sent = pl.pallas_call(
        project_kernel,
        in_specs=[hbm] * 4,
        out_specs=vmem,
        out_shape=jax.ShapeDtypeStruct((wide * narrow, modes, 256), BF16),
        scratch_shapes=[
            pltpu.VMEM((2, 2, modes_first, modes_second, channels), BF16),
            pltpu.VMEM((2, 64, channels), F32),
            pltpu.VMEM((4, channels, 256), BF16),
            pltpu.VMEM((2, 64, 128), F32),
            pltpu.SemaphoreType.DMA((2, parts)),
            pltpu.SemaphoreType.DMA((2,)),
        ],
        name="project",
        compiler_params=pltpu.CompilerParams(vmem_limit_bytes=12 * 2**20),
    )(in_hbm(spectra), in_hbm(out_grads), in_hbm(in_rows), in_hbm(out_rows))
    got = lax.all_to_all(sent, ("wide", "narrow"), split_axis=0, concat_axis=0, tiled=True)
    samples = got.shape[0]
    core = pl.pallas_call(
        product_kernel,
        out_shape=jax.ShapeDtypeStruct((wide * 2 * modes, 128), F32),
        scratch_shapes=[pltpu.VMEM((2, samples * modes, 128), F32)],
        name="product",
        compiler_params=pltpu.CompilerParams(vmem_limit_bytes=8 * 2**20),
    )(got)
    core = core.reshape(wide, 2 * modes, 128)
    core = lax.all_to_all(core, "wide", split_axis=0, concat_axis=0, tiled=True)
    step, new_first, new_second = pl.pallas_call(
        adam_kernel,
        in_specs=[pl.BlockSpec(memory_space=pltpu.SMEM), vmem, vmem, vmem],
        out_specs=[vmem, hbm, hbm],
        out_shape=[
            jax.ShapeDtypeStruct(core.shape, F32),
            jax.ShapeDtypeStruct(first_moment.shape, F32),
            jax.ShapeDtypeStruct(second_moment.shape, F32),
        ],
        scratch_shapes=[
            pltpu.VMEM(first_moment.shape, F32),
            pltpu.VMEM(second_moment.shape, F32),
            pltpu.SemaphoreType.DMA((2,)),
        ],
        name="adam",
        compiler_params=pltpu.CompilerParams(vmem_limit_bytes=4 * 2**20),
    )(mode_rows, core, first_moment, second_moment)
    step = lax.all_to_all(step, "wide", split_axis=0, concat_axis=0, tiled=True)
    flat = weights.reshape(2 * modes, channels, channels)
    new_weights = pl.pallas_call(
        change_kernel,
        in_specs=[vmem] * 4,
        out_specs=hbm,
        out_shape=jax.ShapeDtypeStruct(flat.shape, F32),
        scratch_shapes=[
            pltpu.VMEM((2, 256, channels), BF16),
            pltpu.VMEM((channels, 192), BF16),
            pltpu.VMEM((2, 64, 128), F32),
            pltpu.VMEM(flat.shape, F32),
            pltpu.SemaphoreType.DMA((2 * modes,)),
        ],
        name="change",
        compiler_params=pltpu.CompilerParams(vmem_limit_bytes=14 * 2**20),
    )(step.reshape(wide * 2 * modes, 128), in_rows, out_rows, flat)
    return (new_weights.reshape(weights.shape), new_first, new_second)


def solution(mesh):
    placed = (
        P(None, ("wide", "narrow"), None, None, None),
        P(None, ("wide", "narrow"), None, None, None),
        P(None, "wide", "narrow", None, None),
        P(),
        P(),
        P(),
        P(None, None, "narrow", "wide"),
        P(None, "narrow", "wide"),
    )
    return jax.shard_map(
        local,
        mesh=mesh,
        in_specs=placed,
        out_specs=(
            P(None, "wide", "narrow", None, None),
            P(None, None, "narrow", "wide"),
            P(None, "narrow", "wide"),
        ),
        check_vma=False,
    )
```

```python
import jax
import jax.numpy as jnp
from jax import lax
from jax.experimental import pallas as pl
from jax.experimental.pallas import tpu as pltpu
from jax.sharding import PartitionSpec as P

STEP = 1000
F32 = jnp.float32
BF16 = jnp.bfloat16

GRAD_SCALE = 16.0
FLOOR = 2.0**-12
EDGE = 125.0
SLOPE = 250.0 / 22.2


def encode(v):
    power = jnp.exp2(SLOPE * jnp.log2(1.0 + jnp.abs(v) * (1.0 / FLOOR)) - EDGE)
    return jnp.where(v < 0, -power, power).astype(BF16)


def decode(y):
    size = jnp.exp2((jnp.log2(jnp.abs(y)) + EDGE) * (1.0 / SLOPE)) - 1.0
    return jnp.where(y < 0, -size, size)


def split(v):
    high = v.astype(BF16)
    return high, (v - high.astype(F32)).astype(BF16)


def dot(a, b, dims):
    return lax.dot_general(a, b, (dims, ((), ())), preferred_element_type=F32)


NN = ((1,), (0,))
TN = ((0,), (0,))


def paired_rows(ref, held):
    half = ref.shape[0] // 2
    for c in range(2):
        held[c] = ref[:, c * 128 : c * 128 + 128]
    return jnp.concatenate(
        [
            jnp.concatenate([held[c, pl.ds(k, half, stride=2), :] for c in range(2)], axis=1)
            for k in range(2)
        ],
        axis=0,
    )


def project_kernel(
    x_hbm, g_hbm, in_hbm_ref, out_hbm_ref, sent_ref, sources, rows, factors, held, sems, row_sems
):
    parts = sems.shape[1]
    rows_first = sources.shape[2] // parts
    modes_second, channels = sources.shape[3:]
    narrow = modes_second // 8

    def fetch(side, i):
        at = pl.ds(i * rows_first, rows_first)
        hbm = (x_hbm, g_hbm)[side]
        return pltpu.make_async_copy(hbm.at[:, 0, at], sources.at[side, :, at], sems.at[side, i])

    def fetch_rows(side):
        hbm = (in_hbm_ref, out_hbm_ref)[side]
        return pltpu.make_async_copy(hbm, rows.at[side], row_sems.at[side])

    for side in range(2):
        fetch_rows(side).start()
    for i in range(parts):
        fetch(0, i).start()
    for side in range(2):
        fetch_rows(side).wait()
        factor = GRAD_SCALE * rows[1] if side else paired_rows(rows.at[0], held)
        high, low = split(factor)
        none = jnp.zeros_like(high)
        factors[2 * side] = jnp.concatenate([high, none, low, none], axis=0).T
        factors[2 * side + 1] = jnp.concatenate([none, high, none, low], axis=0).T

    def emit(side, at, count, base):
        modes = count * modes_second
        real = sources[side, 0, at].reshape(modes, channels)
        imag = sources[side, 1, at].reshape(modes, channels)
        both = dot(real, factors[2 * side], NN) + dot(imag, factors[2 * side + 1], NN)
        code = encode(both[:, :128] + both[:, 128:])
        code = code.reshape(count // 2, 2, narrow, 8, 128)
        for w in range(count // 2):
            for n in range(narrow):
                block = jnp.concatenate([code[w, 0, n], code[w, 1, n]], axis=0)
                sent_ref[base + w * narrow + n, :, side * 128 : side * 128 + 128] = block

    @pl.loop(0, parts)
    def _(i):
        fetch(0, i).wait()

        @pl.when(i == 0)
        def _():
            for k in range(parts):
                fetch(1, k).start()

        emit(0, pl.ds(i * rows_first, rows_first), rows_first, i * (rows_first // 2 * narrow))

    for k in range(parts):
        fetch(1, k).wait()
    emit(1, slice(None), parts * rows_first, 0)


def product_kernel(got_ref, core_ref, values):
    samples, modes, lanes = got_ref.shape
    step = 16

    @pl.loop(0, samples // step)
    def _(i):
        block = got_ref[pl.ds(i * step, step)].reshape(step * modes, lanes)
        plain = block.astype(F32)
        for c in range(2):
            values[c, pl.ds(i * step * modes, step * modes), :] = plain[:, c * 128 : c * 128 + 128]

    wide = core_ref.shape[0] // (2 * modes)
    for m in range(modes):
        s_high, s_low = split(decode(values[0, pl.ds(m, samples, stride=modes), :]))
        g_high, g_low = split(decode(values[1, pl.ds(m, samples, stride=modes), :]))
        left = jnp.concatenate([s_high, s_low], axis=1)
        right = jnp.concatenate([g_high, g_low], axis=1)
        full = dot(left, right, TN)
        core = (full[128:, 128:] + full[:128, 128:]) + full[128:, :128] + full[:128, :128]
        real = core[:64, :64] + core[64:, 64:]
        imag = core[:64, 64:] - core[64:, :64]
        for p, part in ((0, real), (1, imag)):
            tile = jnp.concatenate([part[:32], part[32:]], axis=1) * (FLOOR * FLOOR / GRAD_SCALE)
            core_ref[pl.ds(p * modes + m, wide, stride=2 * modes), :] = tile


def adam_kernel(
    mode_ref,
    core_ref,
    first_ref,
    second_ref,
    step_ref,
    first_hbm,
    second_hbm,
    new_first_ref,
    new_second_ref,
    sems,
):
    ranks = mode_ref.shape[0]
    wide = core_ref.shape[0]
    zero = jnp.zeros((8, 128), F32)

    def gather(w, total):
        total = list(total)
        for k in range(2):
            for r in range(ranks):
                factor = mode_ref[r, 2 * w + k]
                for p in range(2):
                    at = p * ranks + r
                    total[at] = total[at] + factor * core_ref[w, pl.ds(16 * p + 8 * k, 8), :]
        return tuple(total)

    total = lax.fori_loop(0, wide, gather, (zero,) * (2 * ranks), unroll=4)
    first_scale = 1.0 / (1.0 - 0.9**STEP)
    second_scale = 1.0 / (1.0 - 0.999**STEP)
    steps = [None] * (2 * ranks)
    for r in range(ranks):
        real, imag = total[r], total[ranks + r]
        second = 0.999 * second_ref[r] + 0.001 * (real * real + imag * imag)
        new_second_ref[r] = second
        below = jnp.sqrt(second * second_scale) + 1e-08
        for p, grad in ((0, real), (1, imag)):
            first = 0.9 * first_ref[p, r] + 0.1 * grad
            new_first_ref[p, r] = first
            steps[p * ranks + r] = first * first_scale / below

    copies = [
        pltpu.make_async_copy(new_first_ref, first_hbm, sems.at[0]),
        pltpu.make_async_copy(new_second_ref, second_hbm, sems.at[1]),
    ]
    for copy in copies:
        copy.start()

    def expand(w, carry):
        for k in range(2):
            parts = [zero, zero]
            for r in range(ranks):
                factor = mode_ref[r, 2 * w + k]
                for p in range(2):
                    parts[p] = parts[p] + factor * steps[p * ranks + r]
            for p in range(2):
                step_ref[w, pl.ds(16 * p + 8 * k, 8), :] = parts[p]
        return carry

    lax.fori_loop(0, wide, expand, 0, unroll=4)
    for copy in copies:
        copy.wait()


def change_kernel(
    step_ref, in_ref, out_ref, weights_ref, new_hbm, right, left, held, changed, sems
):
    modes = weights_ref.shape[0]
    wide = step_ref.shape[0] // modes
    count = 16
    high, low = split(out_ref[...])
    none = jnp.zeros_like(high)
    right[0] = jnp.concatenate([high, high, low, none], axis=0)
    right[1] = jnp.concatenate([high, high, none, low], axis=0)
    high, low = split(0.3 * paired_rows(in_ref, held))
    left[...] = jnp.concatenate([high, high, low], axis=0).T

    def give(m):
        at = pl.ds(2 * m, 2)
        return pltpu.make_async_copy(changed.at[at], new_hbm.at[at], sems.at[m])

    @pl.loop(0, modes // count)
    def _(i):
        rows = jnp.concatenate(
            [step_ref[pl.ds(i * count + j, wide, stride=modes), :] for j in range(count)], axis=0
        )
        high, _ = split(rows)
        coarse = high.astype(F32)
        turned = pltpu.roll(rows - coarse, 64, 1)
        first_half = lax.broadcasted_iota(jnp.int32, rows.shape, 1) < 64
        even, odd = (
            dot(jnp.concatenate([mixed.astype(BF16), high], axis=1), right[k], NN)
            for k, mixed in (
                (0, jnp.where(first_half, coarse, turned)),
                (1, jnp.where(first_half, turned, coarse)),
            )
        )
        for j in range(count):
            m = i * count + j
            mine = slice(j * wide, (j + 1) * wide)
            high, low = split(jnp.concatenate([even[mine], odd[mine]], axis=0))
            stacked = jnp.concatenate([high, low, high], axis=0)
            changed[m] = weights_ref[m] - dot(left[...], stacked, NN)
            if j % 2:
                give(i * (count // 2) + j // 2).start()

    @pl.loop(0, modes // 2)
    def _(m):
        give(m).wait()


def in_hbm(array):
    return pltpu.with_memory_space_constraint(array, pltpu.HBM)


def local(
    spectra, out_grads, weights, mode_factor, in_factor, out_factor, first_moment, second_moment
):
    wide = lax.axis_size("wide")
    narrow = lax.axis_size("narrow")
    _, _, modes_first, modes_second, channels = spectra.shape
    ranks = mode_factor.shape[1]
    modes = (modes_first // wide) * (modes_second // narrow)
    in_rows = in_factor.T
    out_rows = out_factor.T
    mode_rows = mode_factor.T
    parts = 2
    vmem = pl.BlockSpec(memory_space=pltpu.VMEM)
    hbm = pl.BlockSpec(memory_space=pl.ANY)
    sent = pl.pallas_call(
        project_kernel,
        in_specs=[hbm] * 4,
        out_specs=vmem,
        out_shape=jax.ShapeDtypeStruct((wide * narrow, modes, 256), BF16),
        scratch_shapes=[
            pltpu.VMEM((2, 2, modes_first, modes_second, channels), BF16),
            pltpu.VMEM((2, 64, channels), F32),
            pltpu.VMEM((4, channels, 256), BF16),
            pltpu.VMEM((2, 64, 128), F32),
            pltpu.SemaphoreType.DMA((2, parts)),
            pltpu.SemaphoreType.DMA((2,)),
        ],
        name="project",
        compiler_params=pltpu.CompilerParams(vmem_limit_bytes=12 * 2**20),
    )(in_hbm(spectra), in_hbm(out_grads), in_hbm(in_rows), in_hbm(out_rows))
    got = lax.all_to_all(sent, ("wide", "narrow"), split_axis=0, concat_axis=0, tiled=True)
    samples = got.shape[0]
    core = pl.pallas_call(
        product_kernel,
        out_shape=jax.ShapeDtypeStruct((wide * 2 * modes, 128), F32),
        scratch_shapes=[pltpu.VMEM((2, samples * modes, 128), F32)],
        name="product",
        compiler_params=pltpu.CompilerParams(vmem_limit_bytes=8 * 2**20),
    )(got)
    core = core.reshape(wide, 2 * modes, 128)
    core = lax.all_to_all(core, "wide", split_axis=0, concat_axis=0, tiled=True)
    step, new_first, new_second = pl.pallas_call(
        adam_kernel,
        in_specs=[pl.BlockSpec(memory_space=pltpu.SMEM), vmem, vmem, vmem],
        out_specs=[vmem, hbm, hbm],
        out_shape=[
            jax.ShapeDtypeStruct(core.shape, F32),
            jax.ShapeDtypeStruct(first_moment.shape, F32),
            jax.ShapeDtypeStruct(second_moment.shape, F32),
        ],
        scratch_shapes=[
            pltpu.VMEM(first_moment.shape, F32),
            pltpu.VMEM(second_moment.shape, F32),
            pltpu.SemaphoreType.DMA((2,)),
        ],
        name="adam",
        compiler_params=pltpu.CompilerParams(vmem_limit_bytes=4 * 2**20),
    )(mode_rows, core, first_moment, second_moment)
    step = lax.all_to_all(step, "wide", split_axis=0, concat_axis=0, tiled=True)
    flat = weights.reshape(2 * modes, channels, channels)
    new_weights = pl.pallas_call(
        change_kernel,
        in_specs=[vmem] * 4,
        out_specs=hbm,
        out_shape=jax.ShapeDtypeStruct(flat.shape, F32),
        scratch_shapes=[
            pltpu.VMEM((2, 256, channels), BF16),
            pltpu.VMEM((channels, 192), BF16),
            pltpu.VMEM((2, 64, 128), F32),
            pltpu.VMEM(flat.shape, F32),
            pltpu.SemaphoreType.DMA((modes,)),
        ],
        name="change",
        compiler_params=pltpu.CompilerParams(vmem_limit_bytes=14 * 2**20),
    )(step.reshape(wide * 2 * modes, 128), in_rows, out_rows, flat)
    return (new_weights.reshape(weights.shape), new_first, new_second)


def solution(mesh):
    placed = (
        P(None, ("wide", "narrow"), None, None, None),
        P(None, ("wide", "narrow"), None, None, None),
        P(None, "wide", "narrow", None, None),
        P(),
        P(),
        P(),
        P(None, None, "narrow", "wide"),
        P(None, "narrow", "wide"),
    )
    return jax.shard_map(
        local,
        mesh=mesh,
        in_specs=placed,
        out_specs=(
            P(None, "wide", "narrow", None, None),
            P(None, None, "narrow", "wide"),
            P(None, "narrow", "wide"),
        ),
        check_vma=False,
    )
```
